768 devices in a mesh: rep: 16 (over y, x_lo), row: 4 (over x_hi, core), col: 12 (over z).
Axes of the slice: x: 4 (x_hi: 2, x_lo: 2; x = x_hi * 2 + x_lo), y: 8, z: 12, core: 2. Of those that a mesh axis runs over, the one named last changes fastest.
Arguments:
- tokens: bfloat16 [24576, 4096], P('rep', 'row'), may hold values from -6 to 6
- cotangent: bfloat16 [24576, 1536], P(('rep', 'row'), 'col'), may hold values from -4 to 4
- weight: float32 [16, 4096, 1536], P('rep', 'row', 'col'), may hold values from -0.09375 to 0.09375
- first_moment: float32 [16, 4096, 1536], P('rep', 'row', 'col'), may hold values from -6 to 6
- second_moment: float32 [16, 4096, 1536], P('rep', 'row', 'col'), may hold values from 1 to 10
- outer_delta: float32 [16, 7864320], P('rep', ('row', 'col')), may hold values from -6 to 6
- global_params: float32 [2, 7864320], P(None, ('row', 'col')), may hold values from -6 to 6
- outer_moment: float32 [2, 7864320], P(None, ('row', 'col')), may hold values from -6 to 6
- group_slot: int32 [1], replicated, may hold values from 0 to 1
Outputs:
- keys_values: bfloat16 [24576, 1536], P(('rep', 'row'), 'col')
- input_grad: bfloat16 [24576, 4096], P(('rep', 'col'), 'row')
- new_weight: float32 [16, 4096, 1536], P('rep', 'row', 'col')
- new_first: float32 [16, 4096, 1536], P('rep', 'row', 'col')
- new_second: float32 [16, 4096, 1536], P('rep', 'row', 'col')
- new_global: float32 [7864320], P(('row', 'col'))
- new_outer: float32 [7864320], P(('row', 'col'))
The draws below stay inside these ranges and needn't reach their ends.
Inputs may be any that keep to these rules, and one draw needn't show every extreme that they name: `group_slot`: the held group that the outer delta belongs to.
All inputs are finite; a program needn't handle non-finite values.
Results may differ from the reference program's by a relative error of at most 0.015.
Values may be sent and summed in bfloat16 or wider, within the bound.
A program may use at most 64 MiB of HBM per device.

```python
import math
import jax
import jax.numpy as jnp
from jax import lax

DIN = 4096
HD = 128
KVC = 1536
TOK = 1536
SLOTS = 2
GROUP = 7864320
N_REP = 16
N_COL = 12


def block_scale(rng, shape, shards, low, largest):
    level = 1.0
    for axis_at, shards_of in shards:
        draws = jax.random.uniform(jax.random.fold_in(jax.random.fold_in(rng, 6), axis_at), (shards_of,), jnp.float32, low / len(shards), largest / len(shards))
        level = level * jnp.repeat(jnp.exp(draws), shape[axis_at] // shards_of).reshape((-1,) + (1,) * (len(shape) - 1 - axis_at))
    return level


def bell_draw(own_key, shape, scale, bound, cuts=(), dtype=jnp.bfloat16):
    values = scale * jax.random.normal(own_key, shape, jnp.float32)
    if cuts:
        values = values * block_scale(own_key, shape, cuts, -0.22, 0.18)
    return jnp.clip(values, -bound, bound).astype(dtype)


def setup_inputs(seed: int = 0) -> dict:
    seeds = jax.random.split(jax.random.key(seed), 10)
    return {
        "tokens": bell_draw(seeds[0], (N_REP * TOK, DIN), 1.0, 6.0, ((0, 16), (1, 4))),
        "cotangent": bell_draw(seeds[1], (N_REP * TOK, KVC), 0.5, 4.0, ((0, 64), (1, 12))),
        "weight": bell_draw(seeds[2], (N_REP, DIN, KVC), DIN ** -0.5, 0.09375, ((0, 16), (1, 4), (2, 12)), jnp.float32),
        "first_moment": bell_draw(seeds[3], (N_REP, DIN, KVC), 1.0, 6.0, ((0, 16), (1, 4), (2, 12)), jnp.float32),
        "second_moment": jnp.clip(jnp.exp(math.log(10.0) - 2.3025851 * jax.random.uniform(seeds[4], (N_REP, DIN, KVC), jnp.float32) ** block_scale(seeds[4], (N_REP, DIN, KVC), ((0, 16), (1, 4), (2, 12)), -0.2, 0.2)), 1.0, 10.0),
        "outer_delta": bell_draw(seeds[5], (N_REP, GROUP), 1.0, 6.0, ((0, 16), (1, 48)), jnp.float32),
        "global_params": bell_draw(seeds[6], (SLOTS, GROUP), 1.0, 6.0, ((1, 48),), jnp.float32),
        "outer_moment": bell_draw(seeds[7], (SLOTS, GROUP), 1.0, 6.0, ((1, 48),), jnp.float32),
        "group_slot": jax.random.randint(seeds[8], (1,), 0, SLOTS).astype(jnp.int32),
    }


BETA_ONE = 0.9
BETA_TWO = 0.95
INNER_RATE = 0.0003
WEIGHT_DECAY = 0.1
EPSILON = 1e-08
OUTER_RATE = 0.7
NESTEROV = 0.9

def reference(tokens, cotangent, weight, first_moment, second_moment, outer_delta, global_params, outer_moment, group_slot):
    kv_list = []
    dx_list = []
    w_list = []
    m_list = []
    v_list = []
    for replica in range(N_REP):
        row_block = tokens[replica * TOK:(replica + 1) * TOK]
        cot_block = cotangent[replica * TOK:(replica + 1) * TOK]
        weight_bf = weight[replica].astype(jnp.bfloat16)
        kv_list.append(jnp.dot(row_block, weight_bf, preferred_element_type=jnp.float32).astype(jnp.bfloat16))
        gradient = jnp.dot(row_block.T, cot_block, preferred_element_type=jnp.float32)
        total = jnp.zeros((TOK, row_block.shape[1]), jnp.float32)
        for column in range(N_COL):
            piece = jnp.dot(cot_block[:, column * HD:(column + 1) * HD], weight_bf[:, column * HD:(column + 1) * HD].T, preferred_element_type=jnp.float32)
            total = total + lax.optimization_barrier(piece.astype(jnp.bfloat16)).astype(jnp.float32)
        dx_list.append(total.astype(jnp.bfloat16))
        first_new = BETA_ONE * first_moment[replica] + (1.0 - BETA_ONE) * gradient
        second_new = BETA_TWO * second_moment[replica] + (1.0 - BETA_TWO) * gradient * gradient
        w_list.append(weight[replica] - INNER_RATE * (first_new / (jnp.sqrt(second_new) + EPSILON) + WEIGHT_DECAY * weight[replica]))
        m_list.append(first_new)
        v_list.append(second_new)
    average = lax.optimization_barrier(jnp.sum(outer_delta, axis=0)) / N_REP
    chosen = group_slot[0].astype(jnp.int32)
    held_group = lax.dynamic_index_in_dim(global_params, chosen, 0, keepdims=False)
    prior_moment = lax.dynamic_index_in_dim(outer_moment, chosen, 0, keepdims=False)
    new_outer = NESTEROV * prior_moment + average
    new_global = held_group - OUTER_RATE * (average + NESTEROV * new_outer)
    return (jnp.concatenate(kv_list, axis=0), jnp.concatenate(dx_list, axis=0), jnp.stack(w_list), jnp.stack(m_list), jnp.stack(v_list), new_global, new_outer)
```

```python
import functools

import jax
import jax.numpy as jnp
from jax import lax
from jax.experimental import pallas as pl
from jax.experimental.pallas import tpu as pltpu
from jax.sharding import PartitionSpec as P

BETA_ONE = 0.9
BETA_TWO = 0.95
INNER_RATE = 0.0003
WEIGHT_DECAY = 0.1
EPSILON = 1e-08
OUTER_RATE = 0.7
NESTEROV = 0.9

MESH = pl.DeviceIdType.MESH
F32 = jnp.float32
BF16 = jnp.bfloat16
LANES = 128


def step_kernel(
    sizes,
    x_hbm,
    g_hbm,
    w_hbm,
    m_hbm,
    v_hbm,
    od_hbm,
    gp_hbm,
    om_hbm,
    slot_ref,
    kv_o,
    ig_o,
    w_o,
    m_o,
    v_o,
    ng_o,
    no_o,
    x_v,
    g_v,
    w_v,
    wb_v,
    m_v,
    v_v,
    od_v,
    gp_v,
    om_v,
    kvp,
    kvr,
    kvf,
    zs_buf,
    zr_buf,
    ig_v,
    ob,
    xr,
    hs,
    yr,
    of,
    ld,
    st,
    gs,
    gr,
    ks,
    kr,
    zs,
    zr,
    xs,
    xrs,
    ys,
    yrs,
):
    nrep, nrow, ncol = sizes
    ny = nrep // 2
    rep = lax.axis_index("rep")
    row = lax.axis_index("row")
    col = lax.axis_index("col")
    yy = rep // 2
    xlo = rep % 2

    tok = x_v.shape[0]
    feat = x_v.shape[1]
    rtok = tok // nrow
    blk = tok // ncol
    per_row = ncol // nrow
    fh = feat // 2
    orow = od_v.shape[0]
    half = orow // 2
    piece = half // ny

    row_peer = {1: row + 1 - 2 * (row % 2), 2: (row + 2) % 4, 3: 3 - row}
    right = (col + 1) % ncol
    left = (col + ncol - 1) % ncol
    xmate = rep + 1 - 2 * xlo
    ypeer = {d: ((yy + d) % ny) * 2 + xlo for d in range(1, ny)}

    barrier = pltpu.get_barrier_semaphore()
    count = 0
    for d in (1, 2, 3):
        pl.semaphore_signal(barrier, inc=1, device_id=(rep, row_peer[d], col), device_id_type=MESH)
        count += 1
    for c in (left, right):
        pl.semaphore_signal(barrier, inc=1, device_id=(rep, row, c), device_id_type=MESH)
        count += 1
    for d in range(1, ny):
        pl.semaphore_signal(barrier, inc=1, device_id=(ypeer[d], row, col), device_id_type=MESH)
        count += 1
    pl.semaphore_signal(barrier, inc=1, device_id=(xmate, row, col), device_id_type=MESH)
    count += 1

    own_rows = pl.ds(pl.multiple_of(row * rtok, rtok), rtok)
    loads = {
        "w": pltpu.make_async_copy(w_hbm, w_v, ld.at[0]),
        "g": pltpu.make_async_copy(g_hbm, g_v.at[own_rows], ld.at[1]),
        "x": pltpu.make_async_copy(x_hbm, x_v, ld.at[2]),
        "od": pltpu.make_async_copy(od_hbm, od_v, ld.at[3]),
        "m": pltpu.make_async_copy(m_hbm, m_v, ld.at[4]),
        "v": pltpu.make_async_copy(v_hbm, v_v, ld.at[5]),
        "gp0": pltpu.make_async_copy(gp_hbm.at[:, 0, :], gp_v.at[0], ld.at[6]),
        "gp1": pltpu.make_async_copy(gp_hbm.at[:, 1, :], gp_v.at[1], ld.at[7]),
        "om0": pltpu.make_async_copy(om_hbm.at[:, 0, :], om_v.at[0], ld.at[8]),
        "om1": pltpu.make_async_copy(om_hbm.at[:, 1, :], om_v.at[1], ld.at[9]),
    }
    for name in ("w", "g", "x", "od", "m", "v", "gp0", "gp1", "om0", "om1"):
        loads[name].start()

    loads["w"].wait()
    wb_v[...] = w_v[...].astype(BF16)
    pl.semaphore_wait(barrier, count)

    sends = []

    c = (col + ncol // 2 + ncol - per_row * row) % ncol
    if per_row == 3:
        first = jnp.where(c == 0, 0, jnp.where(c == 1, 1, jnp.where(c <= 7, 2, 0)))
        second = jnp.where(first == 1, 0, 1)
        order = (first, second, 3 - first - second)
    else:
        order = tuple(range(per_row))
    for n, j in enumerate(order):
        at = per_row * row + j
        for d in (2, 3, 1):
            copy = pltpu.make_async_remote_copy(
                src_ref=g_hbm.at[pl.ds(pl.multiple_of(j * blk, blk), blk)],
                dst_ref=g_v.at[pl.ds(pl.multiple_of(at * blk, blk), blk)],
                send_sem=gs.at[n, d - 1],
                recv_sem=gr.at[at],
                device_id=(rep, row_peer[d], col),
                device_id_type=MESH,
            )
            copy.start()
            sends.append(copy)

    loads["x"].wait()
    kv_copies = {}
    for d in (2, 3, 1, 0):
        to = row_peer[d] if d else row
        rows = pl.ds(pl.multiple_of(to * rtok, rtok), rtok)
        part = jnp.dot(x_v[rows, :], wb_v[...], preferred_element_type=F32)
        kvp[d] = part.astype(BF16)
        if d:
            copy = pltpu.make_async_remote_copy(
                src_ref=kvp.at[d],
                dst_ref=kvr.at[d - 1],
                send_sem=ks.at[d - 1],
                recv_sem=kr.at[d - 1],
                device_id=(rep, row_peer[d], col),
                device_id_type=MESH,
            )
            copy.start()
            sends.append(copy)
            kv_copies[d] = copy
    loads["g"].wait()

    def await_block(t):
        rows = pl.ds(pl.multiple_of(t * blk, blk), blk)

        @pl.when(t // per_row != row)
        def _():
            pltpu.make_async_remote_copy(
                src_ref=g_v.at[rows],
                dst_ref=g_v.at[rows],
                send_sem=gs.at[0, 0],
                recv_sem=gr.at[t],
                device_id=(rep, row_peer[1], col),
                device_id_type=MESH,
            ).wait_recv()

    waited = set()

    def need(offset):
        if offset % ncol not in waited:
            waited.add(offset % ncol)
            await_block((col + offset + ncol) % ncol)

    def contribution(t, h):
        rows = pl.ds(pl.multiple_of(t * blk, blk), blk)
        return lax.dot_general(
            g_v[rows, :],
            wb_v[h * fh : (h + 1) * fh, :],
            (((1,), (1,)), ((), ())),
            preferred_element_type=F32,
        )

    long, short = ncol // 2, ncol - 1 - ncol // 2
    chains = ((0, 0, long), (1, 1, long), (0, 1, short), (1, 0, short))

    ostores = []
    xcopies = {}
    ycopies = {}
    chunk = 80 if piece % 80 == 0 else piece

    def outer_first():
        loads["od"].wait()

        @pl.loop(0, half // chunk)
        def _(i):
            src = pl.ds(pl.multiple_of((1 - xlo) * half + i * chunk, chunk), chunk)
            dst = pl.ds(pl.multiple_of(i * chunk, chunk), chunk)
            ob[dst, :] = od_v[src, :].astype(BF16)

        copy = pltpu.make_async_remote_copy(
            src_ref=ob,
            dst_ref=xr,
            send_sem=xs.at[0],
            recv_sem=xrs.at[0],
            device_id=(xmate, row, col),
            device_id_type=MESH,
        )
        copy.start()
        sends.append(copy)
        xcopies[0] = copy

    def outer_scatter():
        xcopies[0].wait_recv()

        @pl.loop(0, half // chunk)
        def _(i):
            src = pl.ds(pl.multiple_of(xlo * half + i * chunk, chunk), chunk)
            dst = pl.ds(pl.multiple_of(i * chunk, chunk), chunk)
            hs[dst, :] = (od_v[src, :] + xr[dst, :].astype(F32)).astype(BF16)

        for d in range(1, ny):
            to = (yy + d) % ny
            copy = pltpu.make_async_remote_copy(
                src_ref=hs.at[pl.ds(pl.multiple_of(to * piece, piece), piece)],
                dst_ref=yr.at[d - 1],
                send_sem=ys.at[0, d - 1],
                recv_sem=yrs.at[0, d - 1],
                device_id=(ypeer[d], row, col),
                device_id_type=MESH,
            )
            copy.start()
            sends.append(copy)
            ycopies[0, d] = copy

    def outer_gather():
        mine = pl.ds(pl.multiple_of(yy * piece, piece), piece)
        total = hs[mine, :].astype(F32)
        for d in range(1, ny):
            ycopies[0, d].wait_recv()
            total = total + yr[d - 1].astype(F32)
        of[xlo, mine, :] = total.astype(BF16)
        for d in range(1, ny):
            copy = pltpu.make_async_remote_copy(
                src_ref=of.at[xlo, mine],
                dst_ref=of.at[xlo, mine],
                send_sem=ys.at[1, d - 1],
                recv_sem=yrs.at[1, d - 1],
                device_id=(ypeer[d], row, col),
                device_id_type=MESH,
            )
            copy.start()
            sends.append(copy)

    def outer_last():
        for d in range(1, ny):
            there = pl.ds(pl.multiple_of(((yy + ny - d) % ny) * piece, piece), piece)
            pltpu.make_async_remote_copy(
                src_ref=of.at[xlo, there],
                dst_ref=of.at[xlo, there],
                send_sem=ys.at[1, d - 1],
                recv_sem=yrs.at[1, d - 1],
                device_id=(ypeer[d], row, col),
                device_id_type=MESH,
            ).wait_recv()
        copy = pltpu.make_async_remote_copy(
            src_ref=of.at[xlo],
            dst_ref=of.at[xlo],
            send_sem=xs.at[1],
            recv_sem=xrs.at[1],
            device_id=(xmate, row, col),
            device_id_type=MESH,
        )
        copy.start()
        sends.append(copy)

    def outer_merge():
        pltpu.make_async_remote_copy(
            src_ref=of.at[1 - xlo],
            dst_ref=of.at[1 - xlo],
            send_sem=xs.at[1],
            recv_sem=xrs.at[1],
            device_id=(xmate, row, col),
            device_id_type=MESH,
        ).wait_recv()
        for name in ("gp0", "gp1", "om0", "om1"):
            loads[name].wait()
        second = slot_ref[0] == 1
        for q in range(2):

            @pl.loop(0, half // chunk)
            def _(i):
                here = pl.ds(pl.multiple_of(i * chunk, chunk), chunk)
                full = pl.ds(pl.multiple_of(q * half + i * chunk, chunk), chunk)
                average = of[q, here, :].astype(F32) * (1.0 / nrep)
                prior = jnp.where(second, om_v[1, full, :], om_v[0, full, :])
                held = jnp.where(second, gp_v[1, full, :], gp_v[0, full, :])
                new_outer = NESTEROV * prior + average
                om_v[0, full, :] = new_outer
                gp_v[0, full, :] = held - OUTER_RATE * (average + NESTEROV * new_outer)

        for n, (src, dst) in enumerate(((gp_v, ng_o), (om_v, no_o))):
            copy = pltpu.make_async_copy(src.at[0], dst, st.at[n])
            copy.start()
            ostores.append(copy)

    def keys_values():
        for d in (1, 2, 3):
            kv_copies[d].wait_recv()
        total = kvp[0].astype(F32)
        for d in (1, 2, 3):
            total = total + kvr[d - 1].astype(F32)
        kvf[...] = total.astype(BF16)
        copy = pltpu.make_async_copy(kvf, kv_o, st.at[2])
        copy.start()
        ostores.append(copy)

    gc = 256 if feat % 1024 == 0 else feat // 4

    def optimizer(i):
        def run():
            if i == 0:
                loads["m"].wait()
                loads["v"].wait()
                for j in range(ncol):
                    need(j)
            cols = slice(i * gc, (i + 1) * gc)
            grad = lax.dot_general(
                x_v[:, cols], g_v[...], (((0,), (0,)), ((), ())), preferred_element_type=F32
            )
            first = BETA_ONE * m_v[cols, :] + (1.0 - BETA_ONE) * grad
            second = BETA_TWO * v_v[cols, :] + (1.0 - BETA_TWO) * grad * grad
            m_v[cols, :] = first
            v_v[cols, :] = second
            held = w_v[cols, :]
            w_v[cols, :] = held - INNER_RATE * (first / (jnp.sqrt(second) + EPSILON) + WEIGHT_DECAY * held)
            for n, (src, dst) in enumerate(((w_v, w_o), (m_v, m_o), (v_v, v_o))):
                copy = pltpu.make_async_copy(src.at[cols], dst.at[cols], st.at[3 + 3 * i + n])
                copy.start()
                ostores.append(copy)

        return run

    fill = {
        0: outer_first,
        4: outer_scatter,
        6: keys_values,
        8: outer_gather,
        9: optimizer(0),
        10: optimizer(1),
        11: optimizer(2),
        12: outer_last,
        13: optimizer(3),
        17: outer_merge,
    }
    if ncol != 12:
        plan = list(fill.values())
        fill = {}

    def chain_copy(n, way, k, src):
        return pltpu.make_async_remote_copy(
            src_ref=src,
            dst_ref=zr_buf.at[n, k],
            send_sem=zs.at[n, k],
            recv_sem=zr.at[n, k],
            device_id=(rep, row, right if way == 0 else left),
            device_id_type=MESH,
        )

    slot = 0
    for k in range(long):
        for n, (way, h, length) in enumerate(chains):
            if k >= length:
                continue
            sign = 1 if way == 0 else -1
            need(sign * (length - k))
            part = contribution((col + sign * (length - k) + ncol) % ncol, h)
            if k == 0:
                zs_buf[n] = part.astype(BF16)
                copy = chain_copy(n, way, k, zs_buf.at[n])
            else:
                chain_copy(n, way, k - 1, zr_buf.at[n, k - 1]).wait_recv()
                zr_buf[n, k - 1] = (zr_buf[n, k - 1].astype(F32) + part).astype(BF16)
                copy = chain_copy(n, way, k, zr_buf.at[n, k - 1])
            copy.start()
            sends.append(copy)
            if slot in fill:
                fill[slot]()
            slot += 1
    if ncol != 12:
        for run in plan:
            run()

    need(0)
    for h, pair in ((0, (0, 3)), (1, (1, 2))):
        part = contribution(col, h)
        for n in pair:
            way, _, length = chains[n]
            chain_copy(n, way, length - 1, zr_buf.at[n, length - 1]).wait_recv()
            part = part + zr_buf[n, length - 1].astype(F32)
        ig_v[:, h * fh : (h + 1) * fh] = part.astype(BF16)
    copy = pltpu.make_async_copy(ig_v, ig_o, st.at[15])
    copy.start()
    ostores.append(copy)
    for copy in sends:
        copy.wait_send()
    for copy in ostores:
        copy.wait()


def on_device(sizes, tokens, cotangent, weight, first_moment, second_moment, outer_delta, global_params, outer_moment, group_slot):
    nrep, nrow, ncol = sizes
    tok, feat = tokens.shape
    rtok = cotangent.shape[0]
    blk = tok // ncol
    hd = cotangent.shape[1]
    orow = outer_delta.shape[1] // LANES
    half = orow // 2
    ny = nrep // 2
    piece = half // ny
    long = ncol // 2
    held = global_params.reshape(2, orow, LANES).transpose(1, 0, 2)
    moment = outer_moment.reshape(2, orow, LANES).transpose(1, 0, 2)
    any_ref = pl.BlockSpec(memory_space=pl.ANY)
    vmem = pltpu.VMEM
    dma = pltpu.SemaphoreType.DMA
    shape = jax.ShapeDtypeStruct
    outs = pl.pallas_call(
        functools.partial(step_kernel, sizes),
        out_shape=(
            shape((rtok, hd), BF16),
            shape((blk, feat), BF16),
            shape((feat, hd), F32),
            shape((feat, hd), F32),
            shape((feat, hd), F32),
            shape((orow, LANES), F32),
            shape((orow, LANES), F32),
        ),
        in_specs=[any_ref] * 8 + [pl.BlockSpec(memory_space=pltpu.SMEM)],
        out_specs=(any_ref,) * 7,
        scratch_shapes=[
            vmem((tok, feat), BF16),
            vmem((tok, hd), BF16),
            vmem((feat, hd), F32),
            vmem((feat, hd), BF16),
            vmem((feat, hd), F32),
            vmem((feat, hd), F32),
            vmem((orow, LANES), F32),
            vmem((2, orow, LANES), F32),
            vmem((2, orow, LANES), F32),
            vmem((4, rtok, hd), BF16),
            vmem((3, rtok, hd), BF16),
            vmem((rtok, hd), BF16),
            vmem((4, blk, feat // 2), BF16),
            vmem((4, long, blk, feat // 2), BF16),
            vmem((blk, feat), BF16),
            vmem((half, LANES), BF16),
            vmem((half, LANES), BF16),
            vmem((half, LANES), BF16),
            vmem((max(ny - 1, 1), piece, LANES), BF16),
            vmem((2, half, LANES), BF16),
            dma((10,)),
            dma((16,)),
            dma((ncol // nrow, 3)),
            dma((ncol,)),
            dma((3,)),
            dma((3,)),
            dma((4, long)),
            dma((4, long)),
            dma((2,)),
            dma((2,)),
            dma((2, max(ny - 1, 1))),
            dma((2, max(ny - 1, 1))),
        ],
        compiler_params=pltpu.CompilerParams(collective_id=0, has_side_effects=True),
        name="diloco_step",
    )(
        tokens,
        cotangent,
        weight[0],
        first_moment[0],
        second_moment[0],
        outer_delta.reshape(orow, LANES),
        held,
        moment,
        group_slot,
    )
    keys_values, input_grad, new_weight, new_first, new_second, new_global, new_outer = outs
    return (
        keys_values,
        input_grad,
        new_weight[None],
        new_first[None],
        new_second[None],
        new_global.reshape(-1),
        new_outer.reshape(-1),
    )


def solution(mesh):
    sizes = (mesh.shape["rep"], mesh.shape["row"], mesh.shape["col"])
    in_specs = (
        P("rep", "row"),
        P(("rep", "row"), "col"),
        P("rep", "row", "col"),
        P("rep", "row", "col"),
        P("rep", "row", "col"),
        P("rep", ("row", "col")),
        P(None, ("row", "col")),
        P(None, ("row", "col")),
        P(),
    )
    out_specs = (
        P(("rep", "row"), "col"),
        P(("rep", "col"), "row"),
        P("rep", "row", "col"),
        P("rep", "row", "col"),
        P("rep", "row", "col"),
        P(("row", "col")),
        P(("row", "col")),
    )
    return jax.shard_map(
        functools.partial(on_device, sizes), mesh=mesh, in_specs=in_specs, out_specs=out_specs, check_vma=False
    )
```

```python
import functools

import jax
import jax.numpy as jnp
from jax import lax
from jax.experimental import pallas as pl
from jax.experimental.pallas import tpu as pltpu
from jax.sharding import PartitionSpec as P

BETA_ONE = 0.9
BETA_TWO = 0.95
INNER_RATE = 0.0003
WEIGHT_DECAY = 0.1
EPSILON = 1e-08
OUTER_RATE = 0.7
NESTEROV = 0.9

MESH = pl.DeviceIdType.MESH
F32 = jnp.float32
BF16 = jnp.bfloat16
LANES = 128
PIECES = 2


def step_kernel(
    sizes,
    x_hbm,
    g_hbm,
    w_hbm,
    m_hbm,
    v_hbm,
    od_hbm,
    gp_hbm,
    om_hbm,
    slot_hbm,
    kv_o,
    ig_o,
    w_o,
    m_o,
    v_o,
    ng_o,
    no_o,
    x_v,
    g_v,
    w_v,
    wb_v,
    m_v,
    v_v,
    od_v,
    gp_v,
    om_v,
    kvp,
    kvr,
    kvx,
    zs_buf,
    zr_buf,
    ob,
    xr,
    hs,
    yr,
    of,
    slot_ref,
    ld,
    gs,
    gr,
    ks,
    kr,
    zs,
    zr,
    xs,
    xrs,
    ys,
    yrs,
):
    nrep, nrow, ncol = sizes
    ny = nrep // 2
    rep = lax.axis_index("rep")
    row = lax.axis_index("row")
    col = lax.axis_index("col")
    yy = rep // 2
    xlo = rep % 2

    tok = x_v.shape[0]
    feat = x_v.shape[1]
    rtok = tok // nrow
    blk = tok // ncol
    per_row = ncol // nrow
    fh = feat // PIECES
    orow = od_v.shape[0]
    piece = orow // ny

    row_peer = {1: row + 1 - 2 * (row % 2), 2: (row + 2) % 4, 3: 3 - row}
    right = (col + 1) % ncol
    left = (col + ncol - 1) % ncol
    xmate = rep + 1 - 2 * xlo
    ypeer = {d: ((yy + d) % ny) * 2 + xlo for d in range(1, ny)}

    barrier = pltpu.get_barrier_semaphore()
    count = 0
    for d in (1, 2, 3):
        pl.semaphore_signal(barrier, inc=1, device_id=(rep, row_peer[d], col), device_id_type=MESH)
        count += 1
    for c in (left, right):
        pl.semaphore_signal(barrier, inc=1, device_id=(rep, row, c), device_id_type=MESH)
        count += 1
    for d in range(1, ny):
        pl.semaphore_signal(barrier, inc=1, device_id=(ypeer[d], row, col), device_id_type=MESH)
        count += 1
    pl.semaphore_signal(barrier, inc=1, device_id=(xmate, row, col), device_id_type=MESH)
    count += 1

    own_rows = pl.ds(pl.multiple_of(row * rtok, rtok), rtok)
    loads = {
        "w": pltpu.make_async_copy(w_hbm, w_v, ld.at[0]),
        "g": pltpu.make_async_copy(g_hbm, g_v.at[own_rows], ld.at[1]),
        "x": pltpu.make_async_copy(x_hbm, x_v, ld.at[2]),
        "od": pltpu.make_async_copy(od_hbm, od_v, ld.at[3]),
        "m": pltpu.make_async_copy(m_hbm, m_v, ld.at[4]),
        "v": pltpu.make_async_copy(v_hbm, v_v, ld.at[5]),
        "gp0": pltpu.make_async_copy(gp_hbm.at[:, 0, :], gp_v.at[0], ld.at[6]),
        "gp1": pltpu.make_async_copy(gp_hbm.at[:, 1, :], gp_v.at[1], ld.at[7]),
        "om0": pltpu.make_async_copy(om_hbm.at[:, 0, :], om_v.at[0], ld.at[8]),
        "om1": pltpu.make_async_copy(om_hbm.at[:, 1, :], om_v.at[1], ld.at[9]),
        "slot": pltpu.make_async_copy(slot_hbm, slot_ref, ld.at[10]),
    }
    for name in ("w", "od", "x", "g", "m", "v", "gp0", "gp1", "om0", "om1", "slot"):
        loads[name].start()

    loads["w"].wait()
    wb_v[...] = w_v[...].astype(BF16)
    pl.semaphore_wait(barrier, count)

    sends = []

    def keep(copy):
        sends.append(copy)
        return copy

    def kv_copy(n, src, d):
        return pltpu.make_async_remote_copy(
            src_ref=src,
            dst_ref=kvr.at[n],
            send_sem=ks.at[n],
            recv_sem=kr.at[n],
            device_id=(rep, row_peer[d], col),
            device_id_type=MESH,
        )

    c = (col + ncol // 2 + ncol - per_row * row) % ncol
    if per_row == 3:
        first = jnp.where(c == 0, 0, jnp.where(c == 1, 1, jnp.where(c <= 7, 2, 0)))
        second = jnp.where(first == 1, 0, 1)
        order = (first, second, 3 - first - second)
    else:
        order = tuple(range(per_row))
    for n, j in enumerate(order):
        at = per_row * row + j
        for d in (2, 3, 1):
            copy = pltpu.make_async_remote_copy(
                src_ref=g_hbm.at[pl.ds(pl.multiple_of(j * blk, blk), blk)],
                dst_ref=g_v.at[pl.ds(pl.multiple_of(at * blk, blk), blk)],
                send_sem=gs.at[n, d - 1],
                recv_sem=gr.at[at],
                device_id=(rep, row_peer[d], col),
                device_id_type=MESH,
            )
            copy.start()
            sends.append(copy)


    def await_block(t):
        rows = pl.ds(pl.multiple_of(t * blk, blk), blk)

        @pl.when(t // per_row != row)
        def _():
            pltpu.make_async_remote_copy(
                src_ref=g_v.at[rows],
                dst_ref=g_v.at[rows],
                send_sem=gs.at[0, 0],
                recv_sem=gr.at[t],
                device_id=(rep, row_peer[1], col),
                device_id_type=MESH,
            ).wait_recv()

    waited = set()

    def need(offset):
        if offset % ncol not in waited:
            waited.add(offset % ncol)
            await_block((col + offset + ncol) % ncol)

    def contribution(t, h):
        rows = pl.ds(pl.multiple_of(t * blk, blk), blk)
        return lax.dot_general(
            g_v[rows, :],
            wb_v[h * fh : (h + 1) * fh, :],
            (((1,), (1,)), ((), ())),
            preferred_element_type=F32,
        )

    long, short = ncol // 2, ncol - 1 - ncol // 2
    chains = tuple(
        ((i + n) % 2, i, long if n == 0 else short) for n in range(2) for i in range(PIECES)
    )

    chunk = 80 if piece % 80 == 0 else piece
    mine = pl.ds(pl.multiple_of(yy * piece, piece), piece)

    def y_copy(stage, d, src, dst):
        return pltpu.make_async_remote_copy(
            src_ref=src,
            dst_ref=dst,
            send_sem=ys.at[stage, d - 1],
            recv_sem=yrs.at[stage, d - 1],
            device_id=(ypeer[d], row, col),
            device_id_type=MESH,
        )

    def x_copy():
        return pltpu.make_async_remote_copy(
            src_ref=hs,
            dst_ref=xr,
            send_sem=xs.at[0],
            recv_sem=xrs.at[0],
            device_id=(xmate, row, col),
            device_id_type=MESH,
        )

    def outer_scatter():
        loads["od"].wait()

        @pl.loop(0, orow // chunk)
        def _(i):
            here = pl.ds(pl.multiple_of(i * chunk, chunk), chunk)
            ob[here, :] = od_v[here, :].astype(BF16)

        for d in range(1, ny):
            to = (yy + d) % ny
            rows = pl.ds(pl.multiple_of(to * piece, piece), piece)
            keep(y_copy(0, d, ob.at[rows], yr.at[d - 1])).start()

    def outer_pair():
        total = od_v[mine, :]
        for d in range(1, ny):
            y_copy(0, d, yr.at[d - 1], yr.at[d - 1]).wait_recv()
            total = total + yr[d - 1].astype(F32)
        hs[...] = total.astype(BF16)
        keep(x_copy()).start()

    def outer_gather():
        x_copy().wait_recv()
        of[mine, :] = (hs[...].astype(F32) + xr[...].astype(F32)).astype(BF16)
        for d in range(1, ny):
            keep(y_copy(1, d, of.at[mine], of.at[mine])).start()

    def outer_merge():
        for d in range(1, ny):
            there = pl.ds(pl.multiple_of(((yy + ny - d) % ny) * piece, piece), piece)
            y_copy(1, d, of.at[there], of.at[there]).wait_recv()
        for name in ("gp0", "gp1", "om0", "om1", "slot"):
            loads[name].wait()
        second = slot_ref[0] == 1

        @pl.loop(0, orow // chunk)
        def _(i):
            here = pl.ds(pl.multiple_of(i * chunk, chunk), chunk)
            average = of[here, :].astype(F32) * (1.0 / nrep)
            prior = jnp.where(second, om_v[1, here, :], om_v[0, here, :])
            held = jnp.where(second, gp_v[1, here, :], gp_v[0, here, :])
            new_outer = NESTEROV * prior + average
            no_o[here, :] = new_outer
            ng_o[here, :] = held - OUTER_RATE * (average + NESTEROV * new_outer)

    def kv_parts(which):
        for d in which:
            to = row_peer[d] if d else row
            rows = pl.ds(pl.multiple_of(to * rtok, rtok), rtok)
            part = jnp.dot(x_v[rows, :], wb_v[...], preferred_element_type=F32)
            kvp[d] = part.astype(BF16)
            if d % 2:
                keep(kv_copy(d // 2, kvp.at[d], 1)).start()

    def kv_cross():
        kv_copy(1, kvr.at[1], 1).wait_recv()
        kvx[...] = (kvp[2].astype(F32) + kvr[1].astype(F32)).astype(BF16)
        keep(kv_copy(2, kvx, 2)).start()

    def keys_values():
        kv_copy(0, kvr.at[0], 1).wait_recv()
        kv_copy(2, kvr.at[2], 2).wait_recv()
        total = kvp[0].astype(F32) + kvr[0].astype(F32) + kvr[2].astype(F32)
        kv_o[...] = total.astype(BF16)

    gc = 256 if feat % 1024 == 0 else feat // 4

    def optimizer(i):
        def run():
            if i == 0:
                loads["m"].wait()
                loads["v"].wait()
                for j in range(ncol):
                    need(j)
            cols = slice(i * gc, (i + 1) * gc)
            grad = lax.dot_general(
                x_v[:, cols], g_v[...], (((0,), (0,)), ((), ())), preferred_element_type=F32
            )
            first = BETA_ONE * m_v[cols, :] + (1.0 - BETA_ONE) * grad
            second = BETA_TWO * v_v[cols, :] + (1.0 - BETA_TWO) * grad * grad
            m_o[cols, :] = first
            v_o[cols, :] = second
            held = w_v[cols, :]
            w_o[cols, :] = held - INNER_RATE * (first / (jnp.sqrt(second) + EPSILON) + WEIGHT_DECAY * held)

        return run

    outer_scatter()
    loads["x"].wait()
    kv_parts((3, 1))
    loads["g"].wait()

    fill = {
        (0, 3): functools.partial(kv_parts, (2, 0)),
        (1, 1): kv_cross,
        (1, 3): outer_pair,
        (2, 1): keys_values,
        (2, 2): optimizer(0),
        (2, 3): outer_gather,
        (3, 0): optimizer(1),
        (3, 1): optimizer(2),
        (3, 2): optimizer(3),
        (4, 2): outer_merge,
    }

    def chain_copy(n, way, k, src):
        return pltpu.make_async_remote_copy(
            src_ref=src,
            dst_ref=zr_buf.at[n, k],
            send_sem=zs.at[n, k],
            recv_sem=zr.at[n, k],
            device_id=(rep, row, right if way == 0 else left),
            device_id_type=MESH,
        )

    for k in range(long):
        for n, (way, h, length) in enumerate(chains):
            if k >= length:
                continue
            sign = 1 if way == 0 else -1
            need(sign * (length - k))
            part = contribution((col + sign * (length - k) + ncol) % ncol, h)
            if k == 0:
                zs_buf[n] = part.astype(BF16)
                copy = chain_copy(n, way, k, zs_buf.at[n])
            else:
                chain_copy(n, way, k - 1, zr_buf.at[n, k - 1]).wait_recv()
                zr_buf[n, k - 1] = (zr_buf[n, k - 1].astype(F32) + part).astype(BF16)
                copy = chain_copy(n, way, k, zr_buf.at[n, k - 1])
            copy.start()
            sends.append(copy)
            at = (k, 2 * n // PIECES)
            if 2 * n % PIECES == 0 and at in fill:
                fill.pop(at)()
    for run in fill.values():
        run()

    need(0)
    for h in range(PIECES):
        part = contribution(col, h)
        for n in (h + PIECES, h):
            way, _, length = chains[n]
            chain_copy(n, way, length - 1, zr_buf.at[n, length - 1]).wait_recv()
            part = part + zr_buf[n, length - 1].astype(F32)
        ig_o[:, h * fh : (h + 1) * fh] = part.astype(BF16)
    for copy in sends:
        copy.wait_send()


def write_kernel(*refs):
    copies = [pltpu.make_async_copy(refs[n], refs[7 + n], refs[14].at[n]) for n in range(7)]
    for copy in copies:
        copy.start()
    for copy in copies:
        copy.wait()


def on_device(sizes, tokens, cotangent, weight, first_moment, second_moment, outer_delta, global_params, outer_moment, group_slot):
    nrep, nrow, ncol = sizes
    tok, feat = tokens.shape
    rtok = cotangent.shape[0]
    blk = tok // ncol
    hd = cotangent.shape[1]
    orow = outer_delta.shape[1] // LANES
    ny = nrep // 2
    piece = orow // ny
    long = ncol // 2
    held = global_params.reshape(2, orow, LANES).transpose(1, 0, 2)
    moment = outer_moment.reshape(2, orow, LANES).transpose(1, 0, 2)
    any_ref = pl.BlockSpec(memory_space=pl.ANY)
    vmem = pltpu.VMEM
    dma = pltpu.SemaphoreType.DMA
    shape = jax.ShapeDtypeStruct
    results = (
        shape((rtok, hd), BF16),
        shape((blk, feat), BF16),
        shape((feat, hd), F32),
        shape((feat, hd), F32),
        shape((feat, hd), F32),
        shape((orow, LANES), F32),
        shape((orow, LANES), F32),
    )
    outs = pl.pallas_call(
        functools.partial(step_kernel, sizes),
        out_shape=[vmem(o.shape, o.dtype) for o in results],
        in_specs=[any_ref] * 8 + [pl.BlockSpec(memory_space=pltpu.HBM)],
        out_specs=[pl.BlockSpec(memory_space=vmem)] * 7,
        scratch_shapes=[
            vmem((tok, feat), BF16),
            vmem((tok, hd), BF16),
            vmem((feat, hd), F32),
            vmem((feat, hd), BF16),
            vmem((feat, hd), F32),
            vmem((feat, hd), F32),
            vmem((orow, LANES), F32),
            vmem((2, orow, LANES), F32),
            vmem((2, orow, LANES), F32),
            vmem((4, rtok, hd), BF16),
            vmem((3, rtok, hd), BF16),
            vmem((rtok, hd), BF16),
            vmem((2 * PIECES, blk, feat // PIECES), BF16),
            vmem((2 * PIECES, long, blk, feat // PIECES), BF16),
            vmem((orow, LANES), BF16),
            vmem((piece, LANES), BF16),
            vmem((piece, LANES), BF16),
            vmem((max(ny - 1, 1), piece, LANES), BF16),
            vmem((orow, LANES), BF16),
            pltpu.SMEM((1,), jnp.int32),
            dma((11,)),
            dma((ncol // nrow, 3)),
            dma((ncol,)),
            dma((3,)),
            dma((3,)),
            dma((2 * PIECES, long)),
            dma((2 * PIECES, long)),
            dma((1,)),
            dma((1,)),
            dma((2, max(ny - 1, 1))),
            dma((2, max(ny - 1, 1))),
        ],
        compiler_params=pltpu.CompilerParams(collective_id=0, has_side_effects=True),
        name="diloco_step",
    )(
        tokens,
        cotangent,
        weight[0],
        first_moment[0],
        second_moment[0],
        outer_delta.reshape(orow, LANES),
        held,
        moment,
        group_slot,
    )
    outs = pl.pallas_call(
        write_kernel,
        out_shape=results,
        in_specs=[pl.BlockSpec(memory_space=vmem)] * 7,
        out_specs=[any_ref] * 7,
        scratch_shapes=[dma((7,))],
        name="write_out",
    )(*(pltpu.with_memory_space_constraint(o, vmem) for o in outs))
    keys_values, input_grad, new_weight, new_first, new_second, new_global, new_outer = outs
    return (
        keys_values,
        input_grad,
        new_weight[None],
        new_first[None],
        new_second[None],
        new_global.reshape(-1),
        new_outer.reshape(-1),
    )


def solution(mesh):
    sizes = (mesh.shape["rep"], mesh.shape["row"], mesh.shape["col"])
    in_specs = (
        P("rep", "row"),
        P(("rep", "row"), "col"),
        P("rep", "row", "col"),
        P("rep", "row", "col"),
        P("rep", "row", "col"),
        P("rep", ("row", "col")),
        P(None, ("row", "col")),
        P(None, ("row", "col")),
        P(),
    )
    out_specs = (
        P(("rep", "row"), "col"),
        P(("rep", "col"), "row"),
        P("rep", "row", "col"),
        P("rep", "row", "col"),
        P("rep", "row", "col"),
        P(("row", "col")),
        P(("row", "col")),
    )
    return jax.shard_map(
        functools.partial(on_device, sizes), mesh=mesh, in_specs=in_specs, out_specs=out_specs, check_vma=False
    )
```

```python
import functools

import jax
import jax.numpy as jnp
from jax import lax
from jax.experimental import pallas as pl
from jax.experimental.pallas import tpu as pltpu
from jax.sharding import PartitionSpec as P

BETA_ONE = 0.9
BETA_TWO = 0.95
INNER_RATE = 0.0003
WEIGHT_DECAY = 0.1
EPSILON = 1e-08
OUTER_RATE = 0.7
NESTEROV = 0.9

MESH = pl.DeviceIdType.MESH
F32 = jnp.float32
BF16 = jnp.bfloat16
LANES = 128
PIECES = 2


def step_kernel(
    sizes,
    x_hbm,
    g_hbm,
    w_hbm,
    m_hbm,
    v_hbm,
    od_hbm,
    gp_hbm,
    om_hbm,
    slot_hbm,
    kv_o,
    ig_o,
    w_o,
    m_o,
    v_o,
    ng_o,
    no_o,
    x_v,
    g_v,
    w_v,
    wb_v,
    m_v,
    v_v,
    od_v,
    gp_v,
    om_v,
    kvp,
    kvr,
    kvx,
    zs_buf,
    zr_buf,
    wn_v,
    gx_v,
    ob,
    xr,
    hs,
    yr,
    of,
    slot_ref,
    ld,
    gs,
    gr,
    ks,
    kr,
    zs,
    zr,
    ps,
    pr,
    xs,
    xrs,
    ys,
    yrs,
):
    nrep, nrow, ncol = sizes
    ny = nrep // 2
    rep = lax.axis_index("rep")
    row = lax.axis_index("row")
    col = lax.axis_index("col")
    yy = rep // 2
    xlo = rep % 2

    tok = x_v.shape[0]
    feat = x_v.shape[1]
    rtok = tok // nrow
    blk = tok // ncol
    per_row = ncol // nrow
    fh = feat // PIECES
    orow = od_v.shape[0]
    piece = orow // ny

    row_peer = {1: row + 1 - 2 * (row % 2), 2: (row + 2) % 4, 3: 3 - row}
    right = (col + 1) % ncol
    left = (col + ncol - 1) % ncol
    xmate = rep + 1 - 2 * xlo
    ypeer = {d: ((yy + d) % ny) * 2 + xlo for d in range(1, ny)}

    barrier = pltpu.get_barrier_semaphore()
    count = 0
    for d in (1, 2, 3):
        pl.semaphore_signal(barrier, inc=1, device_id=(rep, row_peer[d], col), device_id_type=MESH)
        count += 1
    for c in (left, right):
        pl.semaphore_signal(barrier, inc=1, device_id=(rep, row, c), device_id_type=MESH)
        count += 1
    for d in range(1, ny):
        pl.semaphore_signal(barrier, inc=1, device_id=(ypeer[d], row, col), device_id_type=MESH)
        count += 1
    pl.semaphore_signal(barrier, inc=1, device_id=(xmate, row, col), device_id_type=MESH)
    count += 1

    own_rows = pl.ds(pl.multiple_of(row * rtok, rtok), rtok)
    loads = {
        "w": pltpu.make_async_copy(w_hbm, w_v, ld.at[0]),
        "g": pltpu.make_async_copy(g_hbm, g_v.at[own_rows], ld.at[1]),
        "x": pltpu.make_async_copy(x_hbm, x_v, ld.at[2]),
        "od": pltpu.make_async_copy(od_hbm, od_v, ld.at[3]),
        "m": pltpu.make_async_copy(m_hbm, m_v, ld.at[4]),
        "v": pltpu.make_async_copy(v_hbm, v_v, ld.at[5]),
        "gp0": pltpu.make_async_copy(gp_hbm.at[:, 0, :], gp_v.at[0], ld.at[6]),
        "gp1": pltpu.make_async_copy(gp_hbm.at[:, 1, :], gp_v.at[1], ld.at[7]),
        "om0": pltpu.make_async_copy(om_hbm.at[:, 0, :], om_v.at[0], ld.at[8]),
        "om1": pltpu.make_async_copy(om_hbm.at[:, 1, :], om_v.at[1], ld.at[9]),
        "slot": pltpu.make_async_copy(slot_hbm, slot_ref, ld.at[10]),
    }
    for name in ("w", "g"):
        loads[name].start()
    pl.semaphore_wait(barrier, count)

    sends = []

    def keep(copy):
        sends.append(copy)
        return copy

    def kv_copy(n, src, d):
        return pltpu.make_async_remote_copy(
            src_ref=src,
            dst_ref=kvr.at[n],
            send_sem=ks.at[n],
            recv_sem=kr.at[n],
            device_id=(rep, row_peer[d], col),
            device_id_type=MESH,
        )

    c = (col + ncol // 2 + ncol - per_row * row) % ncol
    if per_row == 3:
        first = jnp.where(c == 0, 0, jnp.where(c == 1, 1, jnp.where(c <= 7, 2, 0)))
        second = jnp.where(first == 1, 0, 1)
        order = (first, second, 3 - first - second)
    else:
        order = tuple(range(per_row))

    def send_blocks(urgent):
        for n, j in enumerate(order):
            at = per_row * row + j
            far = (at - col - ncol // 2 + 2 * ncol) % ncol
            near = jnp.where(far <= 1, 1, jnp.where(far == ncol - 1, 1, 0))
            for d in (2, 3, 1):
                copy = pltpu.make_async_remote_copy(
                    src_ref=g_hbm.at[pl.ds(pl.multiple_of(j * blk, blk), blk)],
                    dst_ref=g_v.at[pl.ds(pl.multiple_of(at * blk, blk), blk)],
                    send_sem=gs.at[n, d - 1],
                    recv_sem=gr.at[at],
                    device_id=(rep, row_peer[d], col),
                    device_id_type=MESH,
                )
                if urgent:
                    keep(copy)
                pl.when(near == (1 if urgent else 0))(copy.start)

    send_blocks(True)
    for name in ("od", "x", "m", "v", "gp0", "gp1", "om0", "om1", "slot"):
        loads[name].start()
    loads["w"].wait()
    wb_v[...] = w_v[...].astype(BF16)

    def await_block(t):
        rows = pl.ds(pl.multiple_of(t * blk, blk), blk)

        @pl.when(t // per_row != row)
        def _():
            pltpu.make_async_remote_copy(
                src_ref=g_v.at[rows],
                dst_ref=g_v.at[rows],
                send_sem=gs.at[0, 0],
                recv_sem=gr.at[t],
                device_id=(rep, row_peer[1], col),
                device_id_type=MESH,
            ).wait_recv()

    waited = set()

    def need(offset):
        if offset % ncol not in waited:
            waited.add(offset % ncol)
            await_block((col + offset + ncol) % ncol)

    def contribution(t, h):
        rows = pl.ds(pl.multiple_of(t * blk, blk), blk)
        return lax.dot_general(
            g_v[rows, :],
            wb_v[h * fh : (h + 1) * fh, :],
            (((1,), (1,)), ((), ())),
            preferred_element_type=F32,
        )

    hops = ncol // 2 - 1
    chains = ((0, 1), (1, 0), (0, 0), (1, 1))

    def lend_copy(n, way, src, dst):
        return pltpu.make_async_remote_copy(
            src_ref=src,
            dst_ref=dst,
            send_sem=ps.at[n, way],
            recv_sem=pr.at[n, way],
            device_id=(rep, row, right if way == 0 else left),
            device_id_type=MESH,
        )

    def lend_weight(way):
        return lend_copy(0, way, wb_v.at[way * fh : (way + 1) * fh], wn_v.at[way])

    def lend_block(way):
        t = (col + ncol // 2) % ncol
        return lend_copy(1, way, g_v.at[pl.ds(pl.multiple_of(t * blk, blk), blk)], gx_v.at[way])

    chunk = 80 if piece % 80 == 0 else piece
    mine = pl.ds(pl.multiple_of(yy * piece, piece), piece)

    def y_copy(stage, d, src, dst):
        return pltpu.make_async_remote_copy(
            src_ref=src,
            dst_ref=dst,
            send_sem=ys.at[stage, d - 1],
            recv_sem=yrs.at[stage, d - 1],
            device_id=(ypeer[d], row, col),
            device_id_type=MESH,
        )

    def x_copy():
        return pltpu.make_async_remote_copy(
            src_ref=hs,
            dst_ref=xr,
            send_sem=xs.at[0],
            recv_sem=xrs.at[0],
            device_id=(xmate, row, col),
            device_id_type=MESH,
        )

    def outer_scatter():
        loads["od"].wait()

        @pl.loop(0, orow // chunk)
        def _(i):
            here = pl.ds(pl.multiple_of(i * chunk, chunk), chunk)
            ob[here, :] = od_v[here, :].astype(BF16)

        for d in range(1, ny):
            to = (yy + d) % ny
            rows = pl.ds(pl.multiple_of(to * piece, piece), piece)
            keep(y_copy(0, d, ob.at[rows], yr.at[d - 1])).start()

    def outer_pair():
        total = od_v[mine, :]
        for d in range(1, ny):
            y_copy(0, d, yr.at[d - 1], yr.at[d - 1]).wait_recv()
            total = total + yr[d - 1].astype(F32)
        hs[...] = total.astype(BF16)
        keep(x_copy()).start()

    def outer_gather():
        x_copy().wait_recv()
        of[mine, :] = (hs[...].astype(F32) + xr[...].astype(F32)).astype(BF16)
        for d in range(1, ny):
            keep(y_copy(1, d, of.at[mine], of.at[mine])).start()

    def outer_merge():
        for d in range(1, ny):
            there = pl.ds(pl.multiple_of(((yy + ny - d) % ny) * piece, piece), piece)
            y_copy(1, d, of.at[there], of.at[there]).wait_recv()
        for name in ("gp0", "gp1", "om0", "om1", "slot"):
            loads[name].wait()
        second = slot_ref[0] == 1

        @pl.loop(0, orow // chunk)
        def _(i):
            here = pl.ds(pl.multiple_of(i * chunk, chunk), chunk)
            average = of[here, :].astype(F32) * (1.0 / nrep)
            prior = jnp.where(second, om_v[1, here, :], om_v[0, here, :])
            held = jnp.where(second, gp_v[1, here, :], gp_v[0, here, :])
            new_outer = NESTEROV * prior + average
            no_o[here, :] = new_outer
            ng_o[here, :] = held - OUTER_RATE * (average + NESTEROV * new_outer)

    def kv_parts(which):
        if 1 in which:
            loads["x"].wait()
        for d in which:
            to = row_peer[d] if d else row
            rows = pl.ds(pl.multiple_of(to * rtok, rtok), rtok)
            part = jnp.dot(x_v[rows, :], wb_v[...], preferred_element_type=F32)
            kvp[d] = part.astype(BF16)
            if d % 2:
                keep(kv_copy(d // 2, kvp.at[d], 1)).start()

    def kv_cross():
        kv_copy(1, kvr.at[1], 1).wait_recv()
        kvx[...] = (kvp[2].astype(F32) + kvr[1].astype(F32)).astype(BF16)
        keep(kv_copy(2, kvx, 2)).start()

    def keys_values():
        kv_copy(0, kvr.at[0], 1).wait_recv()
        kv_copy(2, kvr.at[2], 2).wait_recv()
        total = kvp[0].astype(F32) + kvr[0].astype(F32) + kvr[2].astype(F32)
        kv_o[...] = total.astype(BF16)

    gc = 256 if feat % 1024 == 0 else feat // 4

    def optimizer(i):
        def run():
            if i == 0:
                loads["m"].wait()
                loads["v"].wait()
                for j in range(ncol):
                    need(j)
            cols = slice(i * gc, (i + 1) * gc)
            grad = lax.dot_general(
                x_v[:, cols], g_v[...], (((0,), (0,)), ((), ())), preferred_element_type=F32
            )
            first = BETA_ONE * m_v[cols, :] + (1.0 - BETA_ONE) * grad
            second = BETA_TWO * v_v[cols, :] + (1.0 - BETA_TWO) * grad * grad
            m_o[cols, :] = first
            v_o[cols, :] = second
            held = w_v[cols, :]
            w_o[cols, :] = held - INNER_RATE * (first / (jnp.sqrt(second) + EPSILON) + WEIGHT_DECAY * held)

        return run

    for way in range(2):
        keep(lend_weight(way)).start()

    outer_scatter()
    loads["g"].wait()
    need(ncol // 2)
    for way in range(2):
        keep(lend_block(way)).start()
    send_blocks(False)

    fill = {
        (0, 3): functools.partial(kv_parts, (3, 1)),
        (1, 0): functools.partial(kv_parts, (2, 0)),
        (1, 2): kv_cross,
        (2, 0): outer_pair,
        (2, 1): keys_values,
        (2, 2): outer_gather,
        (2, 3): optimizer(0),
        (3, 0): optimizer(1),
        (3, 1): optimizer(2),
        (3, 2): optimizer(3),
        (4, 3): outer_merge,
    }

    def chain_copy(n, way, k, src):
        return pltpu.make_async_remote_copy(
            src_ref=src,
            dst_ref=zr_buf.at[n, k],
            send_sem=zs.at[n, k],
            recv_sem=zr.at[n, k],
            device_id=(rep, row, right if way == 0 else left),
            device_id_type=MESH,
        )

    for k in range(hops):
        for n, (way, h) in enumerate(chains):
            away = (1 if way == 0 else -1) * (hops - k)
            need(away)
            part = contribution((col + away + ncol) % ncol, h)
            if k == 0:
                if way == h:
                    lend_weight(way).wait_recv()
                    lend_block(way).wait_recv()
                    part = part + lax.dot_general(
                        gx_v[way], wn_v[way], (((1,), (1,)), ((), ())), preferred_element_type=F32
                    )
                zs_buf[n] = part.astype(BF16)
                copy = chain_copy(n, way, k, zs_buf.at[n])
            else:
                chain_copy(n, way, k - 1, zr_buf.at[n, k - 1]).wait_recv()
                zr_buf[n, k - 1] = (zr_buf[n, k - 1].astype(F32) + part).astype(BF16)
                copy = chain_copy(n, way, k, zr_buf.at[n, k - 1])
            keep(copy).start()
            if (k, n) in fill:
                fill.pop((k, n))()
    for run in fill.values():
        run()

    need(0)
    for h, pair in ((1, (0, 3)), (0, (1, 2))):
        part = contribution(col, h)
        for n in pair:
            chain_copy(n, chains[n][0], hops - 1, zr_buf.at[n, hops - 1]).wait_recv()
            part = part + zr_buf[n, hops - 1].astype(F32)
        ig_o[:, h * fh : (h + 1) * fh] = part.astype(BF16)
    for copy in sends:
        copy.wait_send()


def write_kernel(*refs):
    copies = [pltpu.make_async_copy(refs[n], refs[7 + n], refs[14].at[n]) for n in range(7)]
    for copy in copies:
        copy.start()
    for copy in copies:
        copy.wait()


def on_device(sizes, tokens, cotangent, weight, first_moment, second_moment, outer_delta, global_params, outer_moment, group_slot):
    nrep, nrow, ncol = sizes
    tok, feat = tokens.shape
    rtok = cotangent.shape[0]
    blk = tok // ncol
    hd = cotangent.shape[1]
    orow = outer_delta.shape[1] // LANES
    ny = nrep // 2
    piece = orow // ny
    hops = ncol // 2 - 1
    held = global_params.reshape(2, orow, LANES).transpose(1, 0, 2)
    moment = outer_moment.reshape(2, orow, LANES).transpose(1, 0, 2)
    any_ref = pl.BlockSpec(memory_space=pl.ANY)
    vmem = pltpu.VMEM
    dma = pltpu.SemaphoreType.DMA
    shape = jax.ShapeDtypeStruct
    results = (
        shape((rtok, hd), BF16),
        shape((blk, feat), BF16),
        shape((feat, hd), F32),
        shape((feat, hd), F32),
        shape((feat, hd), F32),
        shape((orow, LANES), F32),
        shape((orow, LANES), F32),
    )
    outs = pl.pallas_call(
        functools.partial(step_kernel, sizes),
        out_shape=[vmem(o.shape, o.dtype) for o in results],
        in_specs=[any_ref] * 8 + [pl.BlockSpec(memory_space=pltpu.HBM)],
        out_specs=[pl.BlockSpec(memory_space=vmem)] * 7,
        scratch_shapes=[
            vmem((tok, feat), BF16),
            vmem((tok, hd), BF16),
            vmem((feat, hd), F32),
            vmem((feat, hd), BF16),
            vmem((feat, hd), F32),
            vmem((feat, hd), F32),
            vmem((orow, LANES), F32),
            vmem((2, orow, LANES), F32),
            vmem((2, orow, LANES), F32),
            vmem((4, rtok, hd), BF16),
            vmem((3, rtok, hd), BF16),
            vmem((rtok, hd), BF16),
            vmem((2 * PIECES, blk, feat // PIECES), BF16),
            vmem((2 * PIECES, hops, blk, feat // PIECES), BF16),
            vmem((2, feat // PIECES, hd), BF16),
            vmem((2, blk, hd), BF16),
            vmem((orow, LANES), BF16),
            vmem((piece, LANES), BF16),
            vmem((piece, LANES), BF16),
            vmem((max(ny - 1, 1), piece, LANES), BF16),
            vmem((orow, LANES), BF16),
            pltpu.SMEM((1,), jnp.int32),
            dma((11,)),
            dma((ncol // nrow, 3)),
            dma((ncol,)),
            dma((3,)),
            dma((3,)),
            dma((2 * PIECES, hops)),
            dma((2 * PIECES, hops)),
            dma((2, 2)),
            dma((2, 2)),
            dma((1,)),
            dma((1,)),
            dma((2, max(ny - 1, 1))),
            dma((2, max(ny - 1, 1))),
        ],
        compiler_params=pltpu.CompilerParams(collective_id=0, has_side_effects=True),
        name="diloco_step",
    )(
        tokens,
        cotangent,
        weight[0],
        first_moment[0],
        second_moment[0],
        outer_delta.reshape(orow, LANES),
        held,
        moment,
        group_slot,
    )
    outs = pl.pallas_call(
        write_kernel,
        out_shape=results,
        in_specs=[pl.BlockSpec(memory_space=vmem)] * 7,
        out_specs=[any_ref] * 7,
        scratch_shapes=[dma((7,))],
        name="write_out",
    )(*(pltpu.with_memory_space_constraint(o, vmem) for o in outs))
    keys_values, input_grad, new_weight, new_first, new_second, new_global, new_outer = outs
    return (
        keys_values,
        input_grad,
        new_weight[None],
        new_first[None],
        new_second[None],
        new_global.reshape(-1),
        new_outer.reshape(-1),
    )


def solution(mesh):
    sizes = (mesh.shape["rep"], mesh.shape["row"], mesh.shape["col"])
    in_specs = (
        P("rep", "row"),
        P(("rep", "row"), "col"),
        P("rep", "row", "col"),
        P("rep", "row", "col"),
        P("rep", "row", "col"),
        P("rep", ("row", "col")),
        P(None, ("row", "col")),
        P(None, ("row", "col")),
        P(),
    )
    out_specs = (
        P(("rep", "row"), "col"),
        P(("rep", "col"), "row"),
        P("rep", "row", "col"),
        P("rep", "row", "col"),
        P("rep", "row", "col"),
        P(("row", "col")),
        P(("row", "col")),
    )
    return jax.shard_map(
        functools.partial(on_device, sizes), mesh=mesh, in_specs=in_specs, out_specs=out_specs, check_vma=False
    )
```

```python
import functools

import jax
import jax.numpy as jnp
from jax import lax
from jax.experimental import pallas as pl
from jax.experimental.pallas import tpu as pltpu
from jax.sharding import PartitionSpec as P

BETA_ONE = 0.9
BETA_TWO = 0.95
INNER_RATE = 0.0003
WEIGHT_DECAY = 0.1
EPSILON = 1e-08
OUTER_RATE = 0.7
NESTEROV = 0.9

MESH = pl.DeviceIdType.MESH
F32 = jnp.float32
BF16 = jnp.bfloat16
LANES = 128
PIECES = 2


def step_kernel(
    sizes,
    x_hbm,
    g_hbm,
    w_hbm,
    m_hbm,
    v_hbm,
    od_hbm,
    gp_hbm,
    om_hbm,
    slot_hbm,
    kv_o,
    ig_o,
    w_o,
    m_o,
    v_o,
    ng_o,
    no_o,
    x_v,
    g_v,
    w_v,
    wb_v,
    m_v,
    v_v,
    od_v,
    gp_v,
    om_v,
    kvp,
    kvr,
    kvx,
    zs_buf,
    zr_buf,
    wn_v,
    gx_v,
    ob,
    xr,
    hs,
    yr,
    of,
    slot_ref,
    ld,
    gs,
    gr,
    ks,
    kr,
    zs,
    zr,
    ps,
    pr,
    xs,
    xrs,
    ys,
    yrs,
):
    nrep, nrow, ncol = sizes
    ny = nrep // 2
    rep = lax.axis_index("rep")
    row = lax.axis_index("row")
    col = lax.axis_index("col")
    yy = rep // 2
    xlo = rep % 2

    tok = x_v.shape[0]
    feat = x_v.shape[1]
    rtok = tok // nrow
    blk = tok // ncol
    per_row = ncol // nrow
    fh = feat // PIECES
    orow = od_v.shape[0]
    piece = orow // ny

    row_peer = {1: row + 1 - 2 * (row % 2), 2: (row + 2) % 4, 3: 3 - row}
    right = (col + 1) % ncol
    left = (col + ncol - 1) % ncol
    xmate = rep + 1 - 2 * xlo
    ypeer = {d: ((yy + d) % ny) * 2 + xlo for d in range(1, ny)}

    barrier = pltpu.get_barrier_semaphore()
    count = 0
    for d in (1, 2, 3):
        pl.semaphore_signal(barrier, inc=1, device_id=(rep, row_peer[d], col), device_id_type=MESH)
        count += 1
    for c in (left, right):
        pl.semaphore_signal(barrier, inc=1, device_id=(rep, row, c), device_id_type=MESH)
        count += 1
    for d in range(1, ny):
        pl.semaphore_signal(barrier, inc=1, device_id=(ypeer[d], row, col), device_id_type=MESH)
        count += 1
    pl.semaphore_signal(barrier, inc=1, device_id=(xmate, row, col), device_id_type=MESH)
    count += 1

    own_rows = pl.ds(pl.multiple_of(row * rtok, rtok), rtok)
    loads = {
        "w": pltpu.make_async_copy(w_hbm, w_v, ld.at[0]),
        "g": pltpu.make_async_copy(g_hbm, g_v.at[own_rows], ld.at[1]),
        "x": pltpu.make_async_copy(x_hbm, x_v, ld.at[2]),
        "od": pltpu.make_async_copy(od_hbm, od_v, ld.at[3]),
        "m": pltpu.make_async_copy(m_hbm, m_v, ld.at[4]),
        "v": pltpu.make_async_copy(v_hbm, v_v, ld.at[5]),
        "gp0": pltpu.make_async_copy(gp_hbm.at[:, 0, :], gp_v.at[0], ld.at[6]),
        "gp1": pltpu.make_async_copy(gp_hbm.at[:, 1, :], gp_v.at[1], ld.at[7]),
        "om0": pltpu.make_async_copy(om_hbm.at[:, 0, :], om_v.at[0], ld.at[8]),
        "om1": pltpu.make_async_copy(om_hbm.at[:, 1, :], om_v.at[1], ld.at[9]),
        "slot": pltpu.make_async_copy(slot_hbm, slot_ref, ld.at[10]),
    }
    for name in ("w", "g"):
        loads[name].start()
    loads["w"].wait()
    wb_v[...] = w_v[...].astype(BF16)
    pl.semaphore_wait(barrier, count)

    sends = []

    def keep(copy):
        sends.append(copy)
        return copy

    def kv_copy(n, src, d):
        return pltpu.make_async_remote_copy(
            src_ref=src,
            dst_ref=kvr.at[n],
            send_sem=ks.at[n],
            recv_sem=kr.at[n],
            device_id=(rep, row_peer[d], col),
            device_id_type=MESH,
        )

    c = (col + ncol // 2 + ncol - per_row * row) % ncol
    if per_row == 3:
        first = jnp.where(c == 0, 0, jnp.where(c == 1, 1, jnp.where(c <= 7, 2, 0)))
        second = jnp.where(first == 1, 0, 1)
        order = (first, second, 3 - first - second)
    else:
        order = tuple(range(per_row))

    def send_blocks(urgent):
        for n, j in enumerate(order):
            at = per_row * row + j
            far = (at - col - ncol // 2 + 2 * ncol) % ncol
            near = jnp.where(far <= 1, 1, jnp.where(far == ncol - 1, 1, 0))
            for d in (2, 3, 1):
                copy = pltpu.make_async_remote_copy(
                    src_ref=g_hbm.at[pl.ds(pl.multiple_of(j * blk, blk), blk)],
                    dst_ref=g_v.at[pl.ds(pl.multiple_of(at * blk, blk), blk)],
                    send_sem=gs.at[n, d - 1],
                    recv_sem=gr.at[at],
                    device_id=(rep, row_peer[d], col),
                    device_id_type=MESH,
                )
                if urgent:
                    keep(copy)
                pl.when(near == (1 if urgent else 0))(copy.start)

    def lend_copy(n, way, src, dst):
        return pltpu.make_async_remote_copy(
            src_ref=src,
            dst_ref=dst,
            send_sem=ps.at[n, way],
            recv_sem=pr.at[n, way],
            device_id=(rep, row, right if way == 0 else left),
            device_id_type=MESH,
        )

    def lend_weight(way):
        return lend_copy(0, way, wb_v.at[way * fh : (way + 1) * fh], wn_v.at[way])

    for way in range(2):
        keep(lend_weight(way)).start()
    send_blocks(True)
    for name in ("od", "x", "m", "v", "gp0", "gp1", "om0", "om1", "slot"):
        loads[name].start()

    def await_block(t):
        rows = pl.ds(pl.multiple_of(t * blk, blk), blk)

        @pl.when(t // per_row != row)
        def _():
            pltpu.make_async_remote_copy(
                src_ref=g_v.at[rows],
                dst_ref=g_v.at[rows],
                send_sem=gs.at[0, 0],
                recv_sem=gr.at[t],
                device_id=(rep, row_peer[1], col),
                device_id_type=MESH,
            ).wait_recv()

    waited = set()

    def need(offset):
        if offset % ncol not in waited:
            waited.add(offset % ncol)
            await_block((col + offset + ncol) % ncol)

    def contribution(t, h):
        rows = pl.ds(pl.multiple_of(t * blk, blk), blk)
        return lax.dot_general(
            g_v[rows, :],
            wb_v[h * fh : (h + 1) * fh, :],
            (((1,), (1,)), ((), ())),
            preferred_element_type=F32,
        )

    hops = ncol // 2 - 1
    chains = ((0, 1), (1, 0), (0, 0), (1, 1))

    def lend_block(way):
        t = (col + ncol // 2) % ncol
        return lend_copy(1, way, g_v.at[pl.ds(pl.multiple_of(t * blk, blk), blk)], gx_v.at[way])

    chunk = 80 if piece % 80 == 0 else piece
    mine = pl.ds(pl.multiple_of(yy * piece, piece), piece)

    def y_copy(stage, d, src, dst):
        return pltpu.make_async_remote_copy(
            src_ref=src,
            dst_ref=dst,
            send_sem=ys.at[stage, d - 1],
            recv_sem=yrs.at[stage, d - 1],
            device_id=(ypeer[d], row, col),
            device_id_type=MESH,
        )

    def x_copy():
        return pltpu.make_async_remote_copy(
            src_ref=hs,
            dst_ref=xr,
            send_sem=xs.at[0],
            recv_sem=xrs.at[0],
            device_id=(xmate, row, col),
            device_id_type=MESH,
        )

    def outer_scatter():
        loads["od"].wait()

        @pl.loop(0, orow // chunk)
        def _(i):
            here = pl.ds(pl.multiple_of(i * chunk, chunk), chunk)
            ob[here, :] = od_v[here, :].astype(BF16)

        for d in range(1, ny):
            to = (yy + d) % ny
            rows = pl.ds(pl.multiple_of(to * piece, piece), piece)
            keep(y_copy(0, d, ob.at[rows], yr.at[d - 1])).start()

    def outer_pair():
        total = od_v[mine, :]
        for d in range(1, ny):
            y_copy(0, d, yr.at[d - 1], yr.at[d - 1]).wait_recv()
            total = total + yr[d - 1].astype(F32)
        hs[...] = total.astype(BF16)
        keep(x_copy()).start()

    def outer_gather():
        x_copy().wait_recv()
        of[mine, :] = (hs[...].astype(F32) + xr[...].astype(F32)).astype(BF16)
        for d in range(1, ny):
            keep(y_copy(1, d, of.at[mine], of.at[mine])).start()

    def outer_merge():
        for d in range(1, ny):
            there = pl.ds(pl.multiple_of(((yy + ny - d) % ny) * piece, piece), piece)
            y_copy(1, d, of.at[there], of.at[there]).wait_recv()
        for name in ("gp0", "gp1", "om0", "om1", "slot"):
            loads[name].wait()
        second = slot_ref[0] == 1

        @pl.loop(0, orow // chunk)
        def _(i):
            here = pl.ds(pl.multiple_of(i * chunk, chunk), chunk)
            average = of[here, :].astype(F32) * (1.0 / nrep)
            prior = jnp.where(second, om_v[1, here, :], om_v[0, here, :])
            held = jnp.where(second, gp_v[1, here, :], gp_v[0, here, :])
            new_outer = NESTEROV * prior + average
            no_o[here, :] = new_outer
            ng_o[here, :] = held - OUTER_RATE * (average + NESTEROV * new_outer)

    def kv_parts(which):
        if 1 in which:
            loads["x"].wait()
        for d in which:
            to = row_peer[d] if d else row
            rows = pl.ds(pl.multiple_of(to * rtok, rtok), rtok)
            part = jnp.dot(x_v[rows, :], wb_v[...], preferred_element_type=F32)
            kvp[d] = part.astype(BF16)
            if d % 2:
                keep(kv_copy(d // 2, kvp.at[d], 1)).start()

    def kv_cross():
        kv_copy(1, kvr.at[1], 1).wait_recv()
        kvx[...] = (kvp[2].astype(F32) + kvr[1].astype(F32)).astype(BF16)
        keep(kv_copy(2, kvx, 2)).start()

    def keys_values():
        kv_copy(0, kvr.at[0], 1).wait_recv()
        kv_copy(2, kvr.at[2], 2).wait_recv()
        total = kvp[0].astype(F32) + kvr[0].astype(F32) + kvr[2].astype(F32)
        kv_o[...] = total.astype(BF16)

    gc = 256 if feat % 1024 == 0 else feat // 4

    def optimizer(i):
        def run():
            if i == 0:
                loads["m"].wait()
                loads["v"].wait()
                for j in range(ncol):
                    need(j)
            cols = slice(i * gc, (i + 1) * gc)
            grad = lax.dot_general(
                x_v[:, cols], g_v[...], (((0,), (0,)), ((), ())), preferred_element_type=F32
            )
            first = BETA_ONE * m_v[cols, :] + (1.0 - BETA_ONE) * grad
            second = BETA_TWO * v_v[cols, :] + (1.0 - BETA_TWO) * grad * grad
            m_o[cols, :] = first
            v_o[cols, :] = second
            held = w_v[cols, :]
            w_o[cols, :] = held - INNER_RATE * (first / (jnp.sqrt(second) + EPSILON) + WEIGHT_DECAY * held)

        return run

    outer_scatter()
    loads["g"].wait()
    need(ncol // 2)
    for way in range(2):
        keep(lend_block(way)).start()
    send_blocks(False)

    fill = {
        (0, 3): functools.partial(kv_parts, (3, 1)),
        (1, 0): functools.partial(kv_parts, (2, 0)),
        (1, 2): kv_cross,
        (2, 0): keys_values,
        (2, 1): outer_pair,
        (2, 2): optimizer(0),
        (2, 3): outer_gather,
        (3, 0): optimizer(1),
        (3, 1): optimizer(2),
        (3, 2): optimizer(3),
        (4, 3): outer_merge,
    }

    def chain_copy(n, way, k, src):
        return pltpu.make_async_remote_copy(
            src_ref=src,
            dst_ref=zr_buf.at[n, k],
            send_sem=zs.at[n, k],
            recv_sem=zr.at[n, k],
            device_id=(rep, row, right if way == 0 else left),
            device_id_type=MESH,
        )

    for k in range(hops):
        for n, (way, h) in enumerate(chains):
            away = (1 if way == 0 else -1) * (hops - k)
            need(away)
            part = contribution((col + away + ncol) % ncol, h)
            if k == 0:
                if way == h:
                    lend_weight(way).wait_recv()
                    lend_block(way).wait_recv()
                    part = part + lax.dot_general(
                        gx_v[way], wn_v[way], (((1,), (1,)), ((), ())), preferred_element_type=F32
                    )
                zs_buf[n] = part.astype(BF16)
                copy = chain_copy(n, way, k, zs_buf.at[n])
            else:
                chain_copy(n, way, k - 1, zr_buf.at[n, k - 1]).wait_recv()
                zr_buf[n, k - 1] = (zr_buf[n, k - 1].astype(F32) + part).astype(BF16)
                copy = chain_copy(n, way, k, zr_buf.at[n, k - 1])
            keep(copy).start()
            if (k, n) in fill:
                fill.pop((k, n))()
    for run in fill.values():
        run()

    need(0)
    for h, pair in ((1, (0, 3)), (0, (1, 2))):
        part = contribution(col, h)
        for n in pair:
            chain_copy(n, chains[n][0], hops - 1, zr_buf.at[n, hops - 1]).wait_recv()
            part = part + zr_buf[n, hops - 1].astype(F32)
        ig_o[:, h * fh : (h + 1) * fh] = part.astype(BF16)
    for copy in sends:
        copy.wait_send()


def write_kernel(*refs):
    copies = []
    for n in (6, 5, 4, 3, 2, 1, 0):
        rows = refs[n].shape[0] // 4
        for i in range(4):
            part = pl.ds(i * rows, rows)
            copies.append(pltpu.make_async_copy(refs[n].at[part], refs[7 + n].at[part], refs[14].at[n, i]))
    for copy in copies:
        copy.start()
    for copy in copies:
        copy.wait()


def on_device(sizes, tokens, cotangent, weight, first_moment, second_moment, outer_delta, global_params, outer_moment, group_slot):
    nrep, nrow, ncol = sizes
    tok, feat = tokens.shape
    rtok = cotangent.shape[0]
    blk = tok // ncol
    hd = cotangent.shape[1]
    orow = outer_delta.shape[1] // LANES
    ny = nrep // 2
    piece = orow // ny
    hops = ncol // 2 - 1
    held = global_params.reshape(2, orow, LANES).transpose(1, 0, 2)
    moment = outer_moment.reshape(2, orow, LANES).transpose(1, 0, 2)
    any_ref = pl.BlockSpec(memory_space=pl.ANY)
    vmem = pltpu.VMEM
    dma = pltpu.SemaphoreType.DMA
    shape = jax.ShapeDtypeStruct
    results = (
        shape((rtok, hd), BF16),
        shape((blk, feat), BF16),
        shape((feat, hd), F32),
        shape((feat, hd), F32),
        shape((feat, hd), F32),
        shape((orow, LANES), F32),
        shape((orow, LANES), F32),
    )
    outs = pl.pallas_call(
        functools.partial(step_kernel, sizes),
        out_shape=[vmem(o.shape, o.dtype) for o in results],
        in_specs=[any_ref] * 8 + [pl.BlockSpec(memory_space=pltpu.HBM)],
        out_specs=[pl.BlockSpec(memory_space=vmem)] * 7,
        scratch_shapes=[
            vmem((tok, feat), BF16),
            vmem((tok, hd), BF16),
            vmem((feat, hd), F32),
            vmem((feat, hd), BF16),
            vmem((feat, hd), F32),
            vmem((feat, hd), F32),
            vmem((orow, LANES), F32),
            vmem((2, orow, LANES), F32),
            vmem((2, orow, LANES), F32),
            vmem((4, rtok, hd), BF16),
            vmem((3, rtok, hd), BF16),
            vmem((rtok, hd), BF16),
            vmem((2 * PIECES, blk, feat // PIECES), BF16),
            vmem((2 * PIECES, hops, blk, feat // PIECES), BF16),
            vmem((2, feat // PIECES, hd), BF16),
            vmem((2, blk, hd), BF16),
            vmem((orow, LANES), BF16),
            vmem((piece, LANES), BF16),
            vmem((piece, LANES), BF16),
            vmem((max(ny - 1, 1), piece, LANES), BF16),
            vmem((orow, LANES), BF16),
            pltpu.SMEM((1,), jnp.int32),
            dma((11,)),
            dma((ncol // nrow, 3)),
            dma((ncol,)),
            dma((3,)),
            dma((3,)),
            dma((2 * PIECES, hops)),
            dma((2 * PIECES, hops)),
            dma((2, 2)),
            dma((2, 2)),
            dma((1,)),
            dma((1,)),
            dma((2, max(ny - 1, 1))),
            dma((2, max(ny - 1, 1))),
        ],
        compiler_params=pltpu.CompilerParams(collective_id=0, has_side_effects=True),
        name="diloco_step",
    )(
        tokens,
        cotangent,
        weight[0],
        first_moment[0],
        second_moment[0],
        outer_delta.reshape(orow, LANES),
        held,
        moment,
        group_slot,
    )
    outs = pl.pallas_call(
        write_kernel,
        out_shape=results,
        in_specs=[pl.BlockSpec(memory_space=vmem)] * 7,
        out_specs=[any_ref] * 7,
        scratch_shapes=[dma((7, 4))],
        name="write_out",
    )(*(pltpu.with_memory_space_constraint(o, vmem) for o in outs))
    keys_values, input_grad, new_weight, new_first, new_second, new_global, new_outer = outs
    return (
        keys_values,
        input_grad,
        new_weight[None],
        new_first[None],
        new_second[None],
        new_global.reshape(-1),
        new_outer.reshape(-1),
    )


def solution(mesh):
    sizes = (mesh.shape["rep"], mesh.shape["row"], mesh.shape["col"])
    in_specs = (
        P("rep", "row"),
        P(("rep", "row"), "col"),
        P("rep", "row", "col"),
        P("rep", "row", "col"),
        P("rep", "row", "col"),
        P("rep", ("row", "col")),
        P(None, ("row", "col")),
        P(None, ("row", "col")),
        P(),
    )
    out_specs = (
        P(("rep", "row"), "col"),
        P(("rep", "col"), "row"),
        P("rep", "row", "col"),
        P("rep", "row", "col"),
        P("rep", "row", "col"),
        P(("row", "col")),
        P(("row", "col")),
    )
    return jax.shard_map(
        functools.partial(on_device, sizes), mesh=mesh, in_specs=in_specs, out_specs=out_specs, check_vma=False
    )
```
